32 devices in a mesh: tm: 16 (over z, y, x), head: 2 (over core).
Axes of the slice: x: 2, y: 2, z: 4, core: 2. Of those that a mesh axis runs over, the one named last changes fastest.
Arguments:
- queries: bfloat16 [2048, 4096], P('tm', 'head'), may hold values from -6 to 6
- keys: bfloat16 [2048, 4096], P('tm', 'head'), may hold values from -6 to 6
- values: bfloat16 [2048, 4096], P('tm', 'head'), may hold values from -6 to 6
- segment: int32 [2048], P('tm'), may hold values from 0 to 1, never falling along the last dimension, each value on 1 to 1792 neighbouring positions
- level_weight: float32 [12, 32, 2048], P(None, 'head', 'tm'), may hold values from 0.16 to 6
- gain: float32 [4096], P('head'), may hold values from 0.1 to 1.9
- grad_out: bfloat16 [2048, 4096], P('tm', 'head'), may hold values from -6 to 6
Outputs:
- normed: bfloat16 [2048, 4096], P('tm', 'head')
- grad_queries: bfloat16 [2048, 4096], P('tm', 'head')
- grad_keys: bfloat16 [2048, 4096], P('tm', 'head')
- grad_values: bfloat16 [2048, 4096], P('tm', 'head')
- grad_level: float32 [12, 32, 2048], P(None, 'head', 'tm')
The draws below stay inside these ranges and needn't reach their ends.
Inputs may be any that keep to these rules, and one draw needn't show every extreme that they name: segment numbers never fall along the sequence; each of the two segments holds 256 to 1792 neighbouring positions.
All inputs are finite; a program needn't handle non-finite values.
Results may differ from the reference program's by a relative error of at most 0.0055.
Values sent between devices are 32-bit elements; how exact they have to be, the bound alone decides.
No kernel may reach another device: no remote copies, remote signals or barrier semaphores. Data moves between devices by JAX's collectives and lax.ppermute only.
A program may use at most 128 MiB of HBM per device.

```python
import math
import jax
import jax.numpy as jnp
import numpy as np
from jax import lax

HEADS = 32
HEAD_DIM = 128
TOK_DEV = 128
TOKENS = 2048
FEAT = 4096
LEVELS = 12
N_TM = 16


def draw_level_weight(key, part):
    ramp = jnp.arange(HEADS, dtype=jnp.float32) / (HEADS - 1) - 0.5
    head_scale = jnp.exp(jnp.log(3.0) * ramp)
    spread = jnp.exp(jax.random.uniform(key, (LEVELS, HEADS, TOKENS), jnp.float32, jnp.log(0.5), jnp.log(2.0)))
    return spread * head_scale[None, :, None]


def steps_of(stream_key, dims, cuts, least, largest):
    def one(axis_at, parts):
        steps = jax.random.uniform(jax.random.fold_in(jax.random.fold_in(stream_key, 6), axis_at), (parts,), jnp.float32, least / len(cuts), largest / len(cuts))
        return jnp.repeat(jnp.exp(steps), dims[axis_at] // parts).reshape((-1,) + (1,) * (len(dims) - axis_at - 1))

    level = one(*cuts[0])
    for cut in cuts[1:]:
        level = level * one(*cut)
    return level


def profile(number_of, total, limit, lean):
    portions = [(1 << 20) // math.isqrt(rank ** lean) + 1 for rank in range(2, number_of + 1)]
    spare, holding = total - limit - (number_of - 1), [1] * (number_of - 1)
    while spare > 0:
        free = [i for i in range(number_of - 1) if holding[i] < limit]
        mass, left = sum([portions[i] for i in free]), spare
        for i in free:
            addition = min(limit - holding[i], max(1, left * portions[i] // mass), spare)
            holding[i] = holding[i] + addition
            spare = spare - addition
    return np.array([limit] + holding)


def uneven(stream_key, number_of, total, reach, skew):
    if number_of == 2:
        one = jax.random.randint(stream_key, (), max(1, total - reach), min(reach, total - 1) + 1)
        return jnp.stack([one, total - one])
    lengths = jnp.asarray(profile(number_of, total, reach, skew), jnp.int32)
    pairs = (number_of - 1) // 2
    giver, taker = lengths[1:1 + 2 * pairs:2], lengths[2:2 + 2 * pairs:2]
    room = jnp.minimum(giver - 1, reach - taker)
    passed = jax.random.randint(jax.random.fold_in(stream_key, 1), (pairs,), 0, 1 << 20) % (room + 1)
    lengths = lengths.at[1:1 + 2 * pairs:2].set(giver - passed).at[2:2 + 2 * pairs:2].set(taker + passed)
    return lengths[jax.random.permutation(jax.random.fold_in(stream_key, 2), number_of)]


def scatter_about(own_key, extent, scale, bound, shards=(), kind=jnp.bfloat16):
    drawn = scale * jax.random.normal(own_key, extent, jnp.float32)
    if shards:
        drawn = drawn * steps_of(own_key, extent, shards, -0.22, 0.18)
    return jnp.clip(drawn, -bound, bound).astype(kind)


def setup_inputs(seed: int = 0) -> dict:
    key_list = jax.random.split(jax.random.key(seed), 8)
    queries = scatter_about(key_list[0], (TOKENS, FEAT), 1.0, 6.0, ((0, 16), (1, 2)))
    keys = scatter_about(key_list[1], (TOKENS, FEAT), 1.0, 6.0, ((0, 16), (1, 2)))
    values = scatter_about(key_list[2], (TOKENS, FEAT), 1.0, 6.0, ((0, 16), (1, 2)))
    segment = jnp.searchsorted(jnp.cumsum(uneven(key_list[3], 2, TOKENS, TOKENS - TOKENS // 8, 2)), jnp.arange(TOKENS), side="right").astype(jnp.int32)
    level_weight = draw_level_weight(jax.random.fold_in(key_list[7], 71), 0)
    gain = jnp.clip(1.0 + 0.18 * jax.random.normal(key_list[5], (FEAT,), jnp.float32), 0.1, 1.9)
    grad_out = scatter_about(key_list[6], (TOKENS, FEAT), 1.0, 6.0, ((0, 16), (1, 2)))
    return {"queries": queries, "keys": keys, "values": values, "segment": segment, "level_weight": level_weight, "gain": gain, "grad_out": grad_out}


EPSILON = 1e-05
PRECISE = lax.Precision.HIGHEST

def level_table(tokens):
    places = jnp.arange(tokens, dtype=jnp.int32)
    crossed = jnp.bitwise_xor(places[:, None], places[None, :])
    levels = jnp.zeros((tokens, tokens), jnp.int32)
    for offset in range(tokens.bit_length() - 1):
        levels = levels + (jnp.right_shift(crossed, offset) > 0).astype(jnp.int32)
    return (levels, places[:, None] >= places[None, :])

def near_weight(block_scaled, block_segment, levels, causal, local_levels):
    same_segment = (block_segment[:, None] == block_segment[None, :]) & causal
    weight = jnp.zeros((block_scaled.shape[1],) + levels.shape, jnp.float32)
    for tier_level in range(local_levels):
        weight = weight + jnp.where(levels == tier_level, block_scaled[tier_level][:, :, None], jnp.float32(0.0))
    return (jnp.where(same_segment[None], weight, jnp.float32(0.0)), same_segment)

def reference(queries, keys, values, segment, level_weight, gain, grad_out):
    tokens = TOK_DEV
    blocks = N_TM
    head_count = HEADS
    head_width = HEAD_DIM
    log_tm = blocks.bit_length() - 1
    local_levels = tokens.bit_length()
    features = head_count * head_width
    levels, causal = level_table(tokens)
    level_scale = jnp.exp2(-jnp.maximum(jnp.arange(LEVELS) - 1, 0).astype(jnp.float32) / 2.0)
    scaled = level_weight * level_scale[:, None, None]
    shape4 = (blocks, tokens, head_count, head_width)
    query_blocks = queries.reshape(shape4)
    key_blocks = keys.reshape(shape4)
    value_blocks = values.reshape(shape4)
    grad_blocks = grad_out.reshape(blocks, tokens, features)
    segment_blocks = segment.reshape(blocks, tokens)
    scaled_blocks = scaled.reshape(LEVELS, head_count, blocks, tokens).transpose(2, 0, 1, 3)
    block_lasts = segment_blocks[:, -1]
    block_numbers = jnp.arange(blocks, dtype=jnp.int32)

    def tail_of(pieces):
        key_block, value_block, block_segment = pieces
        keep_rows = (block_segment == block_segment[-1]).astype(jnp.float32)
        return jnp.einsum('shd,she->hde', key_block.astype(jnp.float32) * keep_rows[:, None, None], value_block.astype(jnp.float32), precision=PRECISE)
    tails = lax.map(tail_of, (key_blocks, value_blocks, segment_blocks))
    group_totals = []
    group_ends = []
    for level_bit in range(log_tm):
        group_size = 2 ** level_bit
        lasts_grouped = block_lasts.reshape(blocks // group_size, group_size)
        end_gates = lasts_grouped[:, -1]
        chosen = (lasts_grouped == end_gates[:, None]).astype(jnp.float32)
        grouped = tails.reshape(blocks // group_size, group_size, head_count, head_width, head_width)
        group_totals.append(jnp.einsum('gm,gmhde->ghde', chosen, grouped, precision=PRECISE))
        group_ends.append(end_gates)

    def block_step(accumulated, pieces):
        query_block, key_block, value_block, grad_block, block_segment, block_scaled, block_index = pieces
        query_float = query_block.astype(jnp.float32)
        key_float = key_block.astype(jnp.float32)
        value_float = value_block.astype(jnp.float32)
        weight, same_segment = near_weight(block_scaled, block_segment, levels, causal, local_levels)
        scores = jnp.einsum('thd,shd->hts', query_float, key_float, precision=PRECISE)
        near_terms = (scores * weight).astype(jnp.bfloat16).astype(jnp.float32)
        mixed_out = jnp.einsum('hts,shd->thd', near_terms, value_float, precision=PRECISE)
        reaches = []
        weighted_all = []
        reads = []
        bucket_all = []
        for level_bit in range(log_tm):
            group_index = jnp.right_shift(block_index, level_bit)
            is_upper = group_index % 2 == 1
            partner = jnp.bitwise_xor(group_index, 1)
            bucket = group_totals[level_bit][partner]
            gate_value = group_ends[level_bit][partner]
            reach_mask = jnp.where(is_upper & (block_segment == gate_value), jnp.float32(1.0), jnp.float32(0.0))
            weighted = reach_mask[:, None] * block_scaled[local_levels + level_bit].T
            remote_read = jnp.einsum('thd,hde->the', query_float, bucket, precision=PRECISE)
            mixed_out = mixed_out + remote_read * weighted[:, :, None]
            reaches.append(reach_mask)
            weighted_all.append(weighted)
            reads.append(remote_read)
            bucket_all.append(bucket)
        flat_out = mixed_out.reshape(tokens, features)
        radius = jnp.sqrt(lax.optimization_barrier(jnp.mean(flat_out * flat_out, axis=1)) + EPSILON)
        normed = (flat_out / radius[:, None] * gain).astype(jnp.bfloat16)
        grad_float = grad_block.astype(jnp.float32)
        project = lax.optimization_barrier(jnp.sum(gain * grad_float * flat_out, axis=1))
        grad_mixed = (gain * grad_float / radius[:, None] - flat_out * (project / (features * radius ** 3))[:, None]).astype(jnp.bfloat16)
        grad_heads = grad_mixed.astype(jnp.float32).reshape(tokens, head_count, head_width)
        grad_near = jnp.einsum('thd,shd->hts', grad_heads, value_float, precision=PRECISE)
        grad_score = (grad_near * weight).astype(jnp.bfloat16).astype(jnp.float32)
        grad_query = jnp.einsum('hts,shd->thd', grad_score, key_float, precision=PRECISE)
        grad_key = jnp.einsum('hts,thd->shd', grad_score, query_float, precision=PRECISE)
        grad_value = jnp.einsum('hts,thd->shd', near_terms, grad_heads, precision=PRECISE)
        masked = jnp.where(same_segment[None], grad_near * scores, jnp.float32(0.0))
        level_rows = [lax.optimization_barrier(jnp.sum(jnp.where(levels == tier_level, masked, jnp.float32(0.0)), axis=2)) for tier_level in range(local_levels)]
        updated = []
        for level_bit in range(log_tm):
            grad_query = grad_query + jnp.einsum('hde,the->thd', bucket_all[level_bit], grad_heads, precision=PRECISE) * weighted_all[level_bit][:, :, None]
            level_rows.append(reaches[level_bit][None, :] * lax.optimization_barrier(jnp.sum(reads[level_bit] * grad_heads, axis=2)).T)
            grad_bucket = jnp.einsum('thd,the->hde', query_float * weighted_all[level_bit][:, :, None], grad_heads, precision=PRECISE)
            updated.append(accumulated[level_bit].at[jnp.right_shift(block_index, level_bit)].add(grad_bucket))
        grad_level = jnp.stack(level_rows) * level_scale[:, None, None]
        return (updated, (normed, grad_query.astype(jnp.bfloat16), grad_key, grad_value, grad_level))
    initial = [jnp.zeros((blocks >> level_bit, head_count, head_width, head_width), jnp.float32) for level_bit in range(log_tm)]
    accumulated, outputs = lax.scan(block_step, initial, (query_blocks, key_blocks, value_blocks, grad_blocks, segment_blocks, scaled_blocks, block_numbers))
    normed, grad_query, partial_key, partial_value, grad_level = outputs

    def finish(pieces):
        key_block, value_block, block_segment, block_index, key_part, value_part = pieces
        grad_tail = jnp.zeros((head_count, head_width, head_width), jnp.float32)
        for level_bit in range(log_tm):
            group_index = jnp.right_shift(block_index, level_bit)
            is_lower = group_index % 2 == 0
            joined = is_lower & (block_segment[-1] == group_ends[level_bit][group_index])
            grad_tail = grad_tail + jnp.where(joined, accumulated[level_bit][jnp.bitwise_xor(group_index, 1)], jnp.float32(0.0))
        keep_rows = (block_segment == block_segment[-1]).astype(jnp.float32)[:, None, None]
        key_grad = key_part + keep_rows * jnp.einsum('hde,she->shd', grad_tail, value_block.astype(jnp.float32), precision=PRECISE)
        value_grad = value_part + keep_rows * jnp.einsum('hde,shd->she', grad_tail, key_block.astype(jnp.float32), precision=PRECISE)
        return (key_grad.astype(jnp.bfloat16), value_grad.astype(jnp.bfloat16))
    grad_keys, grad_values = lax.map(finish, (key_blocks, value_blocks, segment_blocks, block_numbers, partial_key, partial_value))
    total = blocks * tokens
    return (normed.reshape(total, features), grad_query.reshape(total, features), grad_keys.reshape(total, features), grad_values.reshape(total, features), grad_level.transpose(1, 2, 0, 3).reshape(LEVELS, head_count, total))
```

```python
import functools

import jax
import jax.numpy as jnp
from jax import lax
from jax.experimental import pallas as pl
from jax.experimental.pallas import tpu as pltpu
from jax.sharding import PartitionSpec as P

EPSILON = 1e-05
PRECISE = lax.Precision.HIGHEST
F32 = jnp.float32
BF16 = jnp.bfloat16
GATE_ROWS = 8


def level_scale(level):
    return 2.0 ** (-max(level - 1, 0) / 2.0)


def chunk_list(head_count):
    if head_count % 8:
        return [(0, head_count)]
    quarter = head_count // 4
    return [(i * quarter, quarter) for i in range(4)]


def halves(x):
    high = x.astype(BF16)
    return high, (x - high.astype(F32)).astype(BF16)


def dot(a, b, dims):
    return lax.dot_general(a, b, (dims, ((), ())), preferred_element_type=F32)


def dot_wide(a, b, dims):
    high, low = halves(b)
    return dot(a, high, dims) + dot(a, low, dims)


def as_column(row, tokens):
    return jnp.transpose(jnp.broadcast_to(row, (tokens, tokens)))


def row_sums(x):
    ones = jnp.ones((8, x.shape[1]), F32)
    return lax.dot_general(
        ones, x, (((1,), (1,)), ((), ())), precision=PRECISE, preferred_element_type=F32
    )[0:1]


def levels_transposed(tokens):
    source = lax.broadcasted_iota(jnp.int32, (tokens, tokens), 0)
    target = lax.broadcasted_iota(jnp.int32, (tokens, tokens), 1)
    crossed = source ^ target
    levels = jnp.zeros((tokens, tokens), jnp.int32)
    for offset in range(tokens.bit_length() - 1):
        levels = levels + (jnp.right_shift(crossed, offset) > 0).astype(jnp.int32)
    return levels, source <= target


def near_levels(segment_row, tokens):
    levels, causal = levels_transposed(tokens)
    allowed = causal & (as_column(segment_row, tokens) == segment_row)
    return jnp.where(allowed, levels, -1)


def near_weight(levels, weight_ref, head, local_levels):
    weight = jnp.zeros(levels.shape, F32)
    for level in range(local_levels):
        row = weight_ref[level, head : head + 1, :] * level_scale(level)
        weight = jnp.where(levels == level, row, weight)
    return weight


def reach_rows(position_ref, segment_row, gate_refs):
    rows = []
    for bit, gate_ref in enumerate(gate_refs):
        upper = (jnp.right_shift(position_ref[0], bit) & 1) == 1
        hit = jnp.where(segment_row == gate_ref[0:1, :], 1.0, 0.0)
        rows.append(jnp.where(upper, hit, jnp.zeros_like(hit)))
    return rows


def weight_columns(rows, tokens):
    padded = -(-len(rows) // 128) * 128
    stacked = jnp.concatenate(
        rows + [jnp.zeros((padded - len(rows), tokens), F32)], axis=0
    )
    return jnp.transpose(stacked)


def tail_kernel(segment_ref, key_ref, value_ref, out_ref, *, heads, width):
    tokens = key_ref.shape[0]
    segment_row = segment_ref[0:1, :].astype(F32)
    last = segment_row[:, tokens - 1 :]
    keep_row = jnp.where(segment_row == last, 1.0, 0.0)
    for h in range(heads):
        cols = slice(h * width, (h + 1) * width)
        turned = (jnp.transpose(key_ref[:, cols].astype(F32)) * keep_row).astype(BF16)
        out_ref[cols, :] = dot(turned, value_ref[:, cols], ((1,), (0,)))
    out_ref[heads * width :, :] = jnp.broadcast_to(last, (GATE_ROWS, width))


def near_kernel(segment_ref, weight_ref, query_ref, key_ref, value_ref, out_ref, *, first, heads, width):
    tokens = key_ref.shape[0]
    levels = near_levels(segment_ref[0:1, :].astype(F32), tokens)
    for h in range(heads):
        cols = slice(h * width, (h + 1) * width)
        scores = dot(key_ref[:, cols], query_ref[:, cols], ((1,), (1,)))
        weight = near_weight(levels, weight_ref, first + h, tokens.bit_length())
        near = (scores * weight).astype(BF16)
        out_ref[:, cols] = dot(near, value_ref[:, cols], ((0,), (0,)))


def read_kernel(
    position_ref, segment_ref, weight_ref, query_ref, near_ref, gain_ref, grad_ref, sums_ref, *rest, first, heads, width, bits
):
    buckets, (mixed_ref, out_ref) = rest[:bits], rest[bits:]
    tokens = query_ref.shape[0]
    local_levels = tokens.bit_length()
    segment_row = segment_ref[0:1, :].astype(F32)
    gates = [bucket.at[heads * width :, :] for bucket in buckets]
    reaches = reach_rows(position_ref, segment_row, gates)
    rows = [
        reaches[bit] * weight_ref[local_levels + bit, first + h : first + h + 1, :] * level_scale(local_levels + bit)
        for h in range(heads)
        for bit in range(bits)
    ]
    columns = weight_columns(rows, tokens)
    squares = jnp.zeros((tokens, width), F32)
    project = jnp.zeros((tokens, width), F32)
    for h in range(heads):
        cols = slice(h * width, (h + 1) * width)
        mixed = near_ref[:, cols]
        for bit in range(bits):
            at = h * bits + bit
            read = dot_wide(query_ref[:, cols], buckets[bit][cols, :], ((1,), (0,)))
            mixed = mixed + read * columns[:, at : at + 1]
        mixed_ref[:, cols] = mixed
        squares = squares + mixed * mixed
        project = project + gain_ref[0:1, cols] * grad_ref[:, cols].astype(F32) * mixed
    out_ref[0:1, :] = sums_ref[0:1, :] + row_sums(squares)
    out_ref[1:2, :] = sums_ref[1:2, :] + row_sums(project)


def grad_kernel(
    position_ref, segment_ref, weight_ref, sums_ref, query_ref, mixed_ref, gain_ref, grad_ref, *rest, first, heads, width, bits, features
):
    gates = rest[:bits]
    outs = rest[len(rest) - bits - 2 :]
    normed_ref, grad_mixed_ref, bucket_refs = outs[0], outs[1], outs[2:]
    tokens = query_ref.shape[0]
    local_levels = tokens.bit_length()
    segment_row = segment_ref[0:1, :].astype(F32)
    reaches = reach_rows(position_ref, segment_row, gates)
    inverse_row = 1.0 / jnp.sqrt(sums_ref[0:1, :] / features + EPSILON)
    pull_row = sums_ref[1:2, :] / features * inverse_row * inverse_row * inverse_row
    inverse = as_column(inverse_row, tokens)
    pull = as_column(pull_row, tokens)
    for h in range(heads):
        cols = slice(h * width, (h + 1) * width)
        mixed = mixed_ref[:, cols]
        gain = gain_ref[0:1, cols]
        normed_ref[:, cols] = (mixed * inverse * gain).astype(BF16)
        grad_mixed = (gain * grad_ref[:, cols].astype(F32) * inverse - mixed * pull).astype(BF16)
        grad_mixed_ref[:, cols] = grad_mixed
        turned = jnp.transpose(query_ref[:, cols].astype(F32))
        for bit in range(bits):
            row = (
                reaches[bit]
                * weight_ref[local_levels + bit, first + h : first + h + 1, :]
                * level_scale(local_levels + bit)
            )
            high, low = halves(turned * row)
            bucket_refs[bit][cols, :] = dot(high, grad_mixed, ((1,), (0,))) + dot(low, grad_mixed, ((1,), (0,)))


def local_kernel(
    position_ref, segment_ref, weight_ref, query_ref, key_ref, value_ref, grad_mixed_ref, level_in_ref, *rest, first, heads, width, bits
):
    buckets = rest[:bits]
    grad_query_ref, grad_key_ref, grad_value_ref, level_ref = rest[len(rest) - 4 :]
    tokens = query_ref.shape[0]
    local_levels = tokens.bit_length()
    segment_row = segment_ref[0:1, :].astype(F32)
    levels = near_levels(segment_row, tokens)
    gates = [bucket.at[heads * width :, :] for bucket in buckets]
    reaches = reach_rows(position_ref, segment_row, gates)
    rows = [
        reaches[bit] * weight_ref[local_levels + bit, first + h : first + h + 1, :] * level_scale(local_levels + bit)
        for h in range(heads)
        for bit in range(bits)
    ]
    columns = weight_columns(rows, tokens)
    level_ref[...] = level_in_ref[...]
    for h in range(heads):
        cols = slice(h * width, (h + 1) * width)
        at_head = slice(first + h, first + h + 1)
        query, key, value = query_ref[:, cols], key_ref[:, cols], value_ref[:, cols]
        grad_mixed = grad_mixed_ref[:, cols]
        scores = dot(key, query, ((1,), (1,)))
        weight = near_weight(levels, weight_ref, first + h, local_levels)
        near = (scores * weight).astype(BF16)
        grad_near = dot(value, grad_mixed, ((1,), (1,)))
        grad_score = (grad_near * weight).astype(BF16)
        grad_key_ref[:, cols] = dot(grad_score, query, ((1,), (0,)))
        grad_value_ref[:, cols] = dot(near, grad_mixed, ((1,), (0,)))
        product = grad_near * scores
        for level in range(local_levels):
            total = jnp.sum(jnp.where(levels == level, product, 0.0), axis=0, keepdims=True)
            level_ref[level, at_head, :] = total * level_scale(level)
        grad_query = dot(grad_score, key, ((0,), (0,)))
        query_float = query.astype(F32)
        for bit in range(bits):
            at = h * bits + bit
            back = dot_wide(grad_mixed, buckets[bit][cols, :], ((1,), (1,)))
            grad_query = grad_query + back * columns[:, at : at + 1]
            level_ref[local_levels + bit, at_head, :] = (
                row_sums(query_float * back) * reaches[bit] * level_scale(local_levels + bit)
            )
        grad_query_ref[:, cols] = grad_query.astype(BF16)


def finish_kernel(segment_ref, key_ref, value_ref, grad_key_ref, grad_value_ref, staying_ref, incoming_ref, *rest, heads, width):
    out_key_ref, out_value_ref = rest[len(rest) - 2 :]
    tokens = key_ref.shape[0]
    segment_row = segment_ref[0:1, :].astype(F32)
    keep = as_column(jnp.where(segment_row == segment_row[:, tokens - 1 :], 1.0, 0.0), tokens)
    for h in range(heads):
        cols = slice(h * width, (h + 1) * width)
        high, low = halves(staying_ref[cols, :] + incoming_ref[cols, :])
        key, value = key_ref[:, cols], value_ref[:, cols]
        back_key = dot(value, high, ((1,), (1,))) + dot(value, low, ((1,), (1,)))
        back_value = dot(key, high, ((1,), (0,))) + dot(key, low, ((1,), (0,)))
        out_key_ref[:, cols] = (grad_key_ref[:, cols] + keep * back_key).astype(BF16)
        out_value_ref[:, cols] = (grad_value_ref[:, cols] + keep * back_value).astype(BF16)


def whole(shape):
    return pl.BlockSpec(shape, lambda i: (0,) * len(shape))


def per_device(queries, keys, values, segment, level_weight, gain, grad_out):
    tokens, width_all = queries.shape
    total_levels, head_count, _ = level_weight.shape
    width = width_all // head_count
    count = lax.axis_size("tm")
    bits = count.bit_length() - 1
    features = width_all * lax.axis_size("head")
    position = lax.axis_index("tm")
    position_array = position.astype(jnp.int32).reshape(1)
    segment_row = segment.reshape(1, tokens)
    gain_row = gain.reshape(1, width_all)
    chunks = chunk_list(head_count)
    smem = pl.BlockSpec(memory_space=pltpu.SMEM)
    anywhere = pl.BlockSpec(memory_space=pl.ANY)
    seg_spec = whole((1, tokens))
    weight_spec = whole(level_weight.shape)
    wide_shape = (tokens, width_all)

    def cols_spec(first, heads, rows=tokens):
        return pl.BlockSpec((rows, heads * width), lambda i: (0, first // heads))

    def gate_spec(heads):
        return pl.BlockSpec((GATE_ROWS, width), lambda i: (heads * width // GATE_ROWS, 0))

    def call(kernel, name, out_shape, in_specs, out_specs, args, aliases=None):
        return pl.pallas_call(
            kernel,
            grid=(1,),
            in_specs=in_specs,
            out_specs=out_specs,
            out_shape=out_shape,
            input_output_aliases=aliases or {},
            name=name,
        )(*args)

    def shape(dims, kind=F32):
        return jax.ShapeDtypeStruct(dims, kind)

    uppers = [(jnp.right_shift(position, bit) & 1) == 1 for bit in range(bits)]

    def pairs_of(bit):
        if bit == bits - 1:
            if bit > 0:
                return [(i, i ^ (3 << (bit - 1))) for i in range(count // 2)]
            return [(i, i ^ 1) for i in range(count // 2)]
        return [(i, i ^ (1 << bit)) for i in range(count)]

    n_chunks = len(chunks)
    states = [[None] * (bits + 1) for _ in chunks]
    got = [[None] * bits for _ in chunks]
    for c, (first, heads) in enumerate(chunks):
        message = shape((heads * width + GATE_ROWS, width))
        states[c][0] = call(
            functools.partial(tail_kernel, heads=heads, width=width),
            "tails",
            message,
            [seg_spec, cols_spec(first, heads), cols_spec(first, heads)],
            whole(message.shape),
            (segment_row, keys, values),
        )

    def combine(state, arrived, bit, rows):
        same = jnp.where(state[rows : rows + 1] == arrived[rows : rows + 1], 1.0, 0.0)
        is_gate = lax.broadcasted_iota(jnp.int32, state.shape, 0) >= rows
        base = jnp.where(uppers[bit], state, arrived)
        other = jnp.where(uppers[bit], arrived, state)
        return base + jnp.where(is_gate, 0.0, same) * other

    for diagonal in range(n_chunks + bits - 1):
        for c in range(n_chunks):
            bit = diagonal - c
            if not 0 <= bit < bits:
                continue
            rows = chunks[c][1] * width
            with jax.named_scope(f"send_{c}_{bit}"):
                got[c][bit] = lax.ppermute(states[c][bit], "tm", pairs_of(bit))
            if bit < bits - 1:
                states[c][bit + 1] = combine(states[c][bit], got[c][bit], bit, rows)

    near = []
    for first, heads in chunks:
        spec = cols_spec(first, heads)
        near.append(
            call(
                functools.partial(near_kernel, first=first, heads=heads, width=width),
                "near",
                shape((tokens, heads * width)),
                [seg_spec, weight_spec, spec, spec, spec],
                cols_spec(0, heads),
                (segment_row, level_weight, queries, keys, values),
            )
        )
    mixed = []
    sums = jnp.zeros((2, tokens), F32)
    for c, (first, heads) in enumerate(chunks):
        spec = cols_spec(first, heads)
        message = (heads * width + GATE_ROWS, width)
        mixed_chunk, sums = call(
            functools.partial(read_kernel, first=first, heads=heads, width=width, bits=bits),
            "read",
            [shape((tokens, heads * width)), shape((2, tokens))],
            [
                smem,
                seg_spec,
                weight_spec,
                spec,
                cols_spec(0, heads),
                cols_spec(first, heads, 1),
                spec,
                whole((2, tokens)),
            ]
            + [whole(message)] * bits,
            [cols_spec(0, heads), whole((2, tokens))],
            (position_array, segment_row, level_weight, queries, near[c], gain_row, grad_out, sums, *got[c]),
        )
        mixed.append(mixed_chunk)
    sums = lax.psum(sums, "head")

    order = list(range(n_chunks))
    normed = None
    grad_mixed = [None] * n_chunks
    grad_buckets = [None] * n_chunks
    for c in order:
        first, heads = chunks[c]
        spec = cols_spec(first, heads)
        ins = [smem, seg_spec, weight_spec, whole((2, tokens)), spec, cols_spec(0, heads), cols_spec(first, heads, 1), spec]
        ins = ins + [gate_spec(heads)] * bits
        args = (position_array, segment_row, level_weight, sums, queries, mixed[c], gain_row, grad_out, *got[c])
        aliases = {}
        if normed is not None:
            aliases = {len(args): 0}
            ins, args = ins + [anywhere], args + (normed,)
        outs = call(
            functools.partial(grad_kernel, first=first, heads=heads, width=width, bits=bits, features=features),
            "grads",
            [shape(wide_shape, BF16), shape((tokens, heads * width), BF16)] + [shape((heads * width, width))] * bits,
            ins,
            [spec, cols_spec(0, heads)] + [whole((heads * width, width))] * bits,
            args,
            aliases,
        )
        normed, grad_mixed[c], grad_buckets[c] = outs[0], outs[1], outs[2:]

    carried = [None] * n_chunks
    staying = [None] * n_chunks
    for step in range(n_chunks + bits - 1):
        for index, c in enumerate(order):
            bit = bits - 1 - (step - index)
            if not 0 <= bit < bits:
                continue
            heads = chunks[c][1]
            rows = heads * width
            outgoing = grad_buckets[c][bit]
            if bit < bits - 1:
                first_state, first_got = states[c][bit][rows : rows + 1], got[c][bit][rows : rows + 1]
                same = jnp.where(first_state == first_got, 1.0, 0.0)
                outgoing = outgoing + jnp.where(uppers[bit], same, 1.0) * carried[c]
                staying[c] = jnp.where(uppers[bit], 1.0, same) * carried[c]
            with jax.named_scope(f"back_{c}_{bit}"):
                sources = pairs_of(bit)
                if bit == bits - 1:
                    sources = [(b, a) for a, b in sources]
                incoming = lax.ppermute(outgoing, "tm", sources)
            if bit > 0:
                carried[c] = incoming if bit == bits - 1 else staying[c] + incoming
            else:
                carried[c] = incoming

    grad_query = grad_level = None
    near_grads = [None] * n_chunks
    level_in = jnp.zeros(level_weight.shape, F32)
    for c in order:
        first, heads = chunks[c]
        spec = cols_spec(first, heads)
        message = (heads * width + GATE_ROWS, width)
        ins = [smem, seg_spec, weight_spec, spec, spec, spec, cols_spec(0, heads), weight_spec] + [whole(message)] * bits
        args = (position_array, segment_row, level_weight, queries, keys, values, grad_mixed[c], level_in, *got[c])
        aliases = {7: 3}
        if grad_query is not None:
            aliases[len(args)] = 0
            ins, args = ins + [anywhere], args + (grad_query,)
        grad_query, near_key, near_value, level_in = call(
            functools.partial(local_kernel, first=first, heads=heads, width=width, bits=bits),
            "local",
            [shape(wide_shape, BF16), shape((tokens, heads * width)), shape((tokens, heads * width)), shape(level_weight.shape)],
            ins,
            [spec, cols_spec(0, heads), cols_spec(0, heads), weight_spec],
            args,
            aliases,
        )
        near_grads[c] = (near_key, near_value)

    grad_key = grad_value = None
    for c in order:
        first, heads = chunks[c]
        spec = cols_spec(first, heads)
        state = whole((heads * width, width))
        ins = [seg_spec, spec, spec, cols_spec(0, heads), cols_spec(0, heads), state, state]
        args = (segment_row, keys, values, *near_grads[c], staying[c], carried[c])
        aliases = {}
        if grad_key is not None:
            aliases = {len(args): 0, len(args) + 1: 1}
            ins, args = ins + [anywhere, anywhere], args + (grad_key, grad_value)
        grad_key, grad_value = call(
            functools.partial(finish_kernel, heads=heads, width=width),
            "finish",
            [shape(wide_shape, BF16), shape(wide_shape, BF16)],
            ins,
            [spec, spec],
            args,
            aliases,
        )
    return normed, grad_query, grad_key, grad_value, level_in


def solution(mesh):
    placed = (
        P("tm", "head"),
        P("tm", "head"),
        P("tm", "head"),
        P("tm"),
        P(None, "head", "tm"),
        P("head"),
        P("tm", "head"),
    )
    return jax.shard_map(
        per_device,
        mesh=mesh,
        in_specs=placed,
        out_specs=(
            P("tm", "head"),
            P("tm", "head"),
            P("tm", "head"),
            P("tm", "head"),
            P(None, "head", "tm"),
        ),
        check_vma=False,
    )
```

```python
import functools

import jax
import jax.numpy as jnp
from jax import lax
from jax.experimental import pallas as pl
from jax.experimental.pallas import tpu as pltpu
from jax.sharding import PartitionSpec as P

EPSILON = 1e-05
F32 = jnp.float32
BF16 = jnp.bfloat16
GATE_ROWS = 8


def level_scale(level):
    return 2.0 ** (-max(level - 1, 0) / 2.0)


def chunk_list(head_count):
    if head_count % 8:
        return [(0, head_count)]
    quarter = head_count // 4
    return [(i * quarter, quarter) for i in range(4)]


def halves(x):
    high = x.astype(BF16)
    return high, (x - high.astype(F32)).astype(BF16)


def dot(a, b, dims):
    return lax.dot_general(a, b, (dims, ((), ())), preferred_element_type=F32)


def dot_wide(a, b, dims):
    high, low = halves(b)
    return dot(a, high, dims) + dot(a, low, dims)


def as_column(row, tokens):
    return jnp.transpose(jnp.broadcast_to(row, (tokens, tokens)))


def row_sums(x):
    return jnp.sum(jnp.transpose(x), axis=0, keepdims=True)


def levels_transposed(tokens):
    source = lax.broadcasted_iota(jnp.int32, (tokens, tokens), 0)
    target = lax.broadcasted_iota(jnp.int32, (tokens, tokens), 1)
    crossed = source ^ target
    levels = jnp.zeros((tokens, tokens), jnp.int32)
    for offset in range(tokens.bit_length() - 1):
        levels = levels + (jnp.right_shift(crossed, offset) > 0).astype(jnp.int32)
    return levels, source <= target


def near_levels(segment_row, tokens):
    levels, causal = levels_transposed(tokens)
    allowed = causal & (as_column(segment_row, tokens) == segment_row)
    return jnp.where(allowed, levels, -1)


def near_weight(levels, weight_ref, head, local_levels):
    weight = jnp.zeros(levels.shape, F32)
    for level in range(local_levels):
        row = weight_ref[level, head : head + 1, :] * level_scale(level)
        weight = jnp.where(levels == level, row, weight)
    return weight


def reach_rows(position_ref, segment_row, gate_refs):
    rows = []
    for bit, gate_ref in enumerate(gate_refs):
        upper = (jnp.right_shift(position_ref[0], bit) & 1) == 1
        hit = jnp.where(segment_row == gate_ref[0:1, :], 1.0, 0.0)
        rows.append(jnp.where(upper, hit, jnp.zeros_like(hit)))
    return rows


def weight_columns(rows, tokens):
    padded = -(-len(rows) // 128) * 128
    stacked = jnp.concatenate(
        rows + [jnp.zeros((padded - len(rows), tokens), F32)], axis=0
    )
    return jnp.transpose(stacked)


def bit_of(position_ref, bit):
    return jnp.right_shift(position_ref[0], bit) & 1


def tail_kernel(segment_ref, key_ref, value_ref, out_ref, *, first, heads, width):
    tokens = key_ref.shape[0]
    segment_row = segment_ref[0:1, :].astype(F32)
    last = segment_row[:, tokens - 1 :]
    keep_row = jnp.where(segment_row == last, 1.0, 0.0)
    for h in range(heads):
        cols = slice((first + h) * width, (first + h + 1) * width)
        turned = (jnp.transpose(key_ref[:, cols].astype(F32)) * keep_row).astype(BF16)
        out_ref[h * width : (h + 1) * width, :] = dot(turned, value_ref[:, cols], ((1,), (0,)))
    out_ref[heads * width :, :] = jnp.broadcast_to(last, (GATE_ROWS, width))


def combine_kernel(position_ref, state_ref, got_ref, out_ref, *half_refs, bit):
    rows = out_ref.shape[0] - GATE_ROWS
    upper = bit_of(position_ref, bit)
    same = jnp.where(state_ref[rows : rows + 1, :] == got_ref[rows : rows + 1, :], 1.0, 0.0)

    @pl.when(upper == 1)
    def _():
        out_ref[:rows, :] = state_ref[:rows, :] + same * got_ref[:rows, :]
        out_ref[rows:, :] = state_ref[rows:, :]

    @pl.when(upper == 0)
    def _():
        out_ref[:rows, :] = got_ref[:rows, :] + same * state_ref[:rows, :]
        out_ref[rows:, :] = got_ref[rows:, :]

    for half_ref in half_refs:
        half = rows // 2
        start = pl.multiple_of(bit_of(position_ref, 0) * half, 8)
        half_ref[:half, :] = out_ref[pl.ds(start, half), :]
        half_ref[half:, :] = out_ref[rows:, :]


def join_kernel(position_ref, mine_ref, other_ref, out_ref):
    half = mine_ref.shape[0] - GATE_ROWS
    parity = bit_of(position_ref, 0)
    out_ref[pl.ds(pl.multiple_of(parity * half, 8), half), :] = mine_ref[:half, :]
    out_ref[pl.ds(pl.multiple_of((1 - parity) * half, 8), half), :] = other_ref[:half, :]
    out_ref[2 * half :, :] = mine_ref[half:, :]


def near_kernel(segment_ref, weight_ref, query_ref, key_ref, value_ref, out_ref, *, first, heads, width):
    tokens = key_ref.shape[0]
    levels = near_levels(segment_ref[0:1, :].astype(F32), tokens)
    for h in range(heads):
        cols = slice((first + h) * width, (first + h + 1) * width)
        scores = dot(key_ref[:, cols], query_ref[:, cols], ((1,), (1,)))
        weight = near_weight(levels, weight_ref, first + h, tokens.bit_length())
        near = (scores * weight).astype(BF16)
        out_ref[:, h * width : (h + 1) * width] = dot(near, value_ref[:, cols], ((0,), (0,)))


def read_kernel(
    position_ref, segment_ref, weight_ref, query_ref, near_ref, gain_ref, grad_ref, *rest, first, heads, width, bits
):
    buckets, outs = rest[:bits], rest[bits:]
    mixed_ref, out_ref = outs[-2:]
    tokens = query_ref.shape[0]
    local_levels = tokens.bit_length()
    segment_row = segment_ref[0:1, :].astype(F32)
    gates = [bucket.at[heads * width :, :] for bucket in buckets]
    reaches = reach_rows(position_ref, segment_row, gates)
    rows = [
        reaches[bit] * weight_ref[local_levels + bit, first + h : first + h + 1, :] * level_scale(local_levels + bit)
        for h in range(heads)
        for bit in range(bits)
    ]
    columns = weight_columns(rows, tokens)
    squares = jnp.zeros((tokens, width), F32)
    project = jnp.zeros((tokens, width), F32)
    for h in range(heads):
        here = slice(h * width, (h + 1) * width)
        cols = slice((first + h) * width, (first + h + 1) * width)
        mixed = near_ref[:, here]
        for bit in range(bits):
            at = h * bits + bit
            read = dot_wide(query_ref[:, cols], buckets[bit][here, :], ((1,), (0,)))
            mixed = mixed + read * columns[:, at : at + 1]
        mixed_ref[:, here] = mixed
        squares = squares + mixed * mixed
        project = project + gain_ref[0:1, cols] * grad_ref[:, cols].astype(F32) * mixed
    square_row, project_row = row_sums(squares), row_sums(project)
    if len(outs) == 3:
        square_row, project_row = outs[0][0:1, :] + square_row, outs[0][1:2, :] + project_row
    out_ref[0:1, :] = square_row
    out_ref[1:2, :] = project_row


def grad_kernel(
    position_ref, segment_ref, weight_ref, sums_ref, query_ref, mixed_ref, gain_ref, grad_ref, *rest, first, heads, width, bits, features
):
    gates = [ref.at[ref.shape[0] - GATE_ROWS :, :] for ref in rest[:bits]]
    outs = rest[len(rest) - bits - 3 :]
    normed_ref, grad_mixed_ref, send_ref, bucket_refs = outs[0], outs[1], outs[2], outs[3:]
    tokens = query_ref.shape[0]
    local_levels = tokens.bit_length()
    segment_row = segment_ref[0:1, :].astype(F32)
    reaches = reach_rows(position_ref, segment_row, gates)
    inverse_row = 1.0 / jnp.sqrt(sums_ref[0:1, :] / features + EPSILON)
    pull_row = sums_ref[1:2, :] / features * inverse_row * inverse_row * inverse_row
    inverse = as_column(inverse_row, tokens)
    pull = as_column(pull_row, tokens)
    for h in range(heads):
        here = slice(h * width, (h + 1) * width)
        cols = slice((first + h) * width, (first + h + 1) * width)
        mixed = mixed_ref[:, here]
        gain = gain_ref[0:1, cols]
        normed_ref[:, cols] = (mixed * inverse * gain).astype(BF16)
        grad_mixed = (gain * grad_ref[:, cols].astype(F32) * inverse - mixed * pull).astype(BF16)
        grad_mixed_ref[:, here] = grad_mixed
        turned = jnp.transpose(query_ref[:, cols].astype(F32))
        for bit in range(bits):
            row = (
                reaches[bit]
                * weight_ref[local_levels + bit, first + h : first + h + 1, :]
                * level_scale(local_levels + bit)
            )
            high, low = halves(turned * row)
            bucket_refs[bit][here, :] = dot(high, grad_mixed, ((1,), (0,))) + dot(low, grad_mixed, ((1,), (0,)))
    half = heads * width // 2
    start = pl.multiple_of((1 - bit_of(position_ref, 0)) * half, 8)
    send_ref[...] = bucket_refs[bits - 1][pl.ds(start, half), :]


def top_kernel(position_ref, bucket_ref, got_ref, out_ref):
    half = out_ref.shape[0]
    start = pl.multiple_of(bit_of(position_ref, 0) * half, 8)
    out_ref[...] = bucket_ref[pl.ds(start, half), :] + got_ref[...]


def gate_factors(position_ref, state_ref, got_ref, bit):
    rows = state_ref.shape[0] - GATE_ROWS
    same = jnp.where(state_ref[rows : rows + 1, :] == got_ref[rows : rows + 1, :], 1.0, 0.0)
    upper = jnp.full_like(same, bit_of(position_ref, bit).astype(F32))
    return upper * same + (1.0 - upper), upper + (1.0 - upper) * same


def back_first_kernel(position_ref, state_ref, got_ref, bucket_ref, half_ref, out_ref, stay_ref, *, bit):
    send, stay = gate_factors(position_ref, state_ref, got_ref, bit)
    half = half_ref.shape[0]
    parity = bit_of(position_ref, 0)
    mine = pl.ds(pl.multiple_of(parity * half, 8), half)
    other = pl.ds(pl.multiple_of((1 - parity) * half, 8), half)
    out_ref[mine, :] = bucket_ref[mine, :] + send * half_ref[...]
    out_ref[other, :] = bucket_ref[other, :]
    stay_ref[mine, :] = stay * half_ref[...]
    stay_ref[other, :] = jnp.zeros_like(half_ref)


def back_kernel(position_ref, state_ref, got_ref, bucket_ref, before_ref, incoming_ref, out_ref, stay_ref, *, bit):
    send, stay = gate_factors(position_ref, state_ref, got_ref, bit)
    carried = before_ref[...] + incoming_ref[...]
    out_ref[...] = bucket_ref[...] + send * carried
    stay_ref[...] = stay * carried


def local_kernel(
    position_ref, segment_ref, weight_ref, query_ref, key_ref, value_ref, grad_mixed_ref, *rest, first, heads, width, bits
):
    buckets = rest[:bits]
    grad_query_ref, grad_key_ref, grad_value_ref, level_ref = rest[len(rest) - 4 :]
    tokens = query_ref.shape[0]
    local_levels = tokens.bit_length()
    segment_row = segment_ref[0:1, :].astype(F32)
    levels = near_levels(segment_row, tokens)
    gates = [bucket.at[heads * width :, :] for bucket in buckets]
    reaches = reach_rows(position_ref, segment_row, gates)
    for h in range(heads):
        here = slice(h * width, (h + 1) * width)
        cols = slice((first + h) * width, (first + h + 1) * width)
        at_head = slice(first + h, first + h + 1)
        query, key, value = query_ref[:, cols], key_ref[:, cols], value_ref[:, cols]
        grad_mixed = grad_mixed_ref[:, here]
        scores = dot(key, query, ((1,), (1,)))
        weight = near_weight(levels, weight_ref, first + h, local_levels)
        near = (scores * weight).astype(BF16)
        grad_near = dot(value, grad_mixed, ((1,), (1,)))
        grad_score = (grad_near * weight).astype(BF16)
        grad_key_ref[:, here] = dot(grad_score, query, ((1,), (0,)))
        grad_value_ref[:, here] = dot(near, grad_mixed, ((1,), (0,)))
        product = grad_near * scores
        for level in range(local_levels):
            total = jnp.sum(jnp.where(levels == level, product, 0.0), axis=0, keepdims=True)
            level_ref[level, at_head, :] = total * level_scale(level)
        grad_query = dot(key, grad_score, ((0,), (0,)))
        query_turned = jnp.transpose(query.astype(F32))
        for bit in range(bits):
            high, low = halves(buckets[bit][here, :])
            back = dot(high, grad_mixed, ((1,), (1,))) + dot(low, grad_mixed, ((1,), (1,)))
            reach = reaches[bit] * level_scale(local_levels + bit)
            grad_query = grad_query + back * (reach * weight_ref[local_levels + bit, at_head, :])
            level_ref[local_levels + bit, at_head, :] = reach * jnp.sum(query_turned * back, axis=0, keepdims=True)
        grad_query_ref[:, cols] = jnp.transpose(grad_query).astype(BF16)


def finish_kernel(
    segment_ref, key_ref, value_ref, grad_key_ref, grad_value_ref, staying_ref, incoming_ref, *rest, first, heads, width
):
    out_key_ref, out_value_ref = rest[len(rest) - 2 :]
    tokens = key_ref.shape[0]
    segment_row = segment_ref[0:1, :].astype(F32)
    keep = as_column(jnp.where(segment_row == segment_row[:, tokens - 1 :], 1.0, 0.0), tokens)
    for h in range(heads):
        here = slice(h * width, (h + 1) * width)
        cols = slice((first + h) * width, (first + h + 1) * width)
        high, low = halves(staying_ref[here, :] + incoming_ref[here, :])
        key, value = key_ref[:, cols], value_ref[:, cols]
        back_key = dot(value, high, ((1,), (1,))) + dot(value, low, ((1,), (1,)))
        back_value = dot(key, high, ((1,), (0,))) + dot(key, low, ((1,), (0,)))
        out_key_ref[:, cols] = (grad_key_ref[:, here] + keep * back_key).astype(BF16)
        out_value_ref[:, cols] = (grad_value_ref[:, here] + keep * back_value).astype(BF16)


def call(kernel, name, outs, args, aliases=None, **static):
    position, *arrays = args
    specs = [pl.BlockSpec(memory_space=pltpu.VMEM)] * len(arrays)
    arrays = [pltpu.with_memory_space_constraint(a, pltpu.VMEM) for a in arrays]
    if position is not None:
        specs, arrays = [pl.BlockSpec(memory_space=pltpu.SMEM)] + specs, [position] + arrays
    result = pl.pallas_call(
        functools.partial(kernel, **static),
        in_specs=specs,
        out_specs=[pl.BlockSpec(memory_space=pltpu.VMEM)] * len(outs),
        out_shape=[pltpu.VMEM(dims, kind) for dims, kind in outs],
        input_output_aliases=aliases or {},
        compiler_params=pltpu.CompilerParams(vmem_limit_bytes=4 << 20),
        name=name,
    )(*arrays)
    return result


def per_device(queries, keys, values, segment, level_weight, gain, grad_out):
    tokens, width_all = queries.shape
    _, head_count, _ = level_weight.shape
    width = width_all // head_count
    count = lax.axis_size("tm")
    bits = count.bit_length() - 1
    top = bits - 1
    features = width_all * lax.axis_size("head")
    position = lax.axis_index("tm").astype(jnp.int32).reshape(1)
    segment_row = segment.reshape(1, tokens)
    gain_row = gain.reshape(1, width_all)
    chunks = chunk_list(head_count)
    n_chunks = len(chunks)
    wide = ((tokens, width_all), BF16)

    swap_all = [[(i, i ^ (1 << bit)) for i in range(count)] for bit in range(bits)]
    climb = [(i, i + count // 2) for i in range(count // 2)]
    descend = [(b, a) for a, b in climb]
    swap_upper = [(i, i ^ 1) for i in range(count // 2, count)]

    states = [[None] * bits for _ in chunks]
    got = [[None] * bits for _ in chunks]
    half_state = [None] * n_chunks
    half_got = [None] * n_chunks
    for c, (first, heads) in enumerate(chunks):
        message = ((heads * width + GATE_ROWS, width), F32)
        (states[c][0],) = call(
            tail_kernel, "tails", [message], (None, segment_row, keys, values), first=first, heads=heads, width=width
        )

    def forward_step(c, stage):
        heads = chunks[c][1]
        message = ((heads * width + GATE_ROWS, width), F32)
        half = ((heads * width // 2 + GATE_ROWS, width), F32)
        if stage < top:
            got[c][stage] = lax.ppermute(states[c][stage], "tm", swap_all[stage])
            outs = [message] + ([half] if stage == top - 1 else [])
            result = call(
                combine_kernel, "combine", outs, (position, states[c][stage], got[c][stage]), bit=stage
            )
            states[c][stage + 1] = result[0]
            half_state[c] = result[-1]
        elif stage == top:
            half_got[c] = lax.ppermute(half_state[c], "tm", climb)
        else:
            other = lax.ppermute(half_got[c], "tm", swap_upper)
            (got[c][top],) = call(join_kernel, "join", [message], (position, half_got[c], other))

    for diagonal in range(n_chunks + bits):
        for c in range(n_chunks):
            if 0 <= diagonal - c <= bits:
                forward_step(c, diagonal - c)

    near = []
    for first, heads in chunks:
        near += call(
            near_kernel,
            "near",
            [((tokens, heads * width), F32)],
            (None, segment_row, level_weight, queries, keys, values),
            first=first,
            heads=heads,
            width=width,
        )
    mixed = []
    sums = ()
    for c, (first, heads) in enumerate(chunks):
        mixed_chunk, row_pair = call(
            read_kernel,
            "read",
            [((tokens, heads * width), F32), ((2, tokens), F32)],
            (position, segment_row, level_weight, queries, near[c], gain_row, grad_out, *got[c], *sums),
            first=first,
            heads=heads,
            width=width,
            bits=bits,
        )
        mixed.append(mixed_chunk)
        sums = (row_pair,)
    totals = lax.psum(sums[0], "head")

    normed = ()
    grad_mixed = [None] * n_chunks
    grad_buckets = [None] * n_chunks
    to_neighbour = [None] * n_chunks
    for c, (first, heads) in enumerate(chunks):
        rows = heads * width
        args = (position, segment_row, level_weight, totals, queries, mixed[c], gain_row, grad_out, *got[c], *normed)
        outs = call(
            grad_kernel,
            "grads",
            [wide, ((tokens, rows), BF16), ((rows // 2, width), F32)] + [((rows, width), F32)] * bits,
            args,
            {len(args) - 1: 0} if normed else None,
            first=first,
            heads=heads,
            width=width,
            bits=bits,
            features=features,
        )
        normed = (outs[0],)
        grad_mixed[c], to_neighbour[c], grad_buckets[c] = outs[1], outs[2], outs[3:]

    half_sum = [None] * n_chunks
    staying = [None] * n_chunks
    carried = [None] * n_chunks

    def backward_step(c, stage):
        rows = chunks[c][1] * width
        full = ((rows, width), F32)
        if stage == 0:
            arrived = lax.ppermute(to_neighbour[c], "tm", swap_upper)
            (half_sum[c],) = call(
                top_kernel, "top", [((rows // 2, width), F32)], (position, grad_buckets[c][top], arrived)
            )
        elif stage == 1:
            half = lax.ppermute(half_sum[c], "tm", descend)
            bit = top - 1
            outgoing, staying[c] = call(
                back_first_kernel,
                "back",
                [full, full],
                (position, states[c][bit], got[c][bit], grad_buckets[c][bit], half),
                bit=bit,
            )
            carried[c] = outgoing
        else:
            bit = top + 1 - stage
            incoming = lax.ppermute(carried[c], "tm", swap_all[bit])
            if bit == 0:
                carried[c] = incoming
                return
            carried[c], staying[c] = call(
                back_kernel,
                "back",
                [full, full],
                (position, states[c][bit - 1], got[c][bit - 1], grad_buckets[c][bit - 1], staying[c], incoming),
                bit=bit - 1,
            )

    grad_query = level_out = None
    near_grads = [None] * n_chunks

    def local_step(c):
        nonlocal grad_query, level_out
        first, heads = chunks[c]
        rows = heads * width
        args = (position, segment_row, level_weight, queries, keys, values, grad_mixed[c], *got[c], carried[c])
        aliases = None
        if grad_query is not None:
            aliases = {len(args): 0, len(args) + 1: 3}
            args = args + (grad_query, level_out)
        grad_query, near_key, near_value, level_out = call(
            local_kernel,
            "local",
            [wide, ((tokens, rows), F32), ((tokens, rows), F32), (level_weight.shape, F32)],
            args,
            aliases,
            first=first,
            heads=heads,
            width=width,
            bits=bits,
        )
        near_grads[c] = (near_key, near_value)

    for step in range(n_chunks + bits):
        for c in range(n_chunks):
            if 0 <= step - c <= bits:
                backward_step(c, step - c)
                if step - c == 1:
                    local_step(c)

    grad_key = grad_value = None
    for c, (first, heads) in enumerate(chunks):
        args = (None, segment_row, keys, values, *near_grads[c], staying[c], carried[c])
        aliases = None
        if grad_key is not None:
            aliases = {len(args) - 1: 0, len(args): 1}
            args = args + (grad_key, grad_value)
        grad_key, grad_value = call(
            finish_kernel, "finish", [wide, wide], args, aliases, first=first, heads=heads, width=width
        )
    return normed[0], grad_query, grad_key, grad_value, level_out


def solution(mesh):
    placed = (
        P("tm", "head"),
        P("tm", "head"),
        P("tm", "head"),
        P("tm"),
        P(None, "head", "tm"),
        P("head"),
        P("tm", "head"),
    )
    return jax.shard_map(
        per_device,
        mesh=mesh,
        in_specs=placed,
        out_specs=(
            P("tm", "head"),
            P("tm", "head"),
            P("tm", "head"),
            P("tm", "head"),
            P(None, "head", "tm"),
        ),
        check_vma=False,
    )
```

```python
import functools

import jax
import jax.numpy as jnp
from jax import lax
from jax.experimental import pallas as pl
from jax.experimental.pallas import tpu as pltpu
from jax.sharding import PartitionSpec as P

EPSILON = 1e-05
F32 = jnp.float32
BF16 = jnp.bfloat16
GATE_ROWS = 8


def level_scale(level):
    return 2.0 ** (-max(level - 1, 0) / 2.0)


def chunk_list(head_count):
    if head_count % 8:
        return [(0, head_count)]
    quarter = head_count // 4
    return [(i * quarter, quarter) for i in range(4)]


def halves(x):
    high = x.astype(BF16)
    return high, (x - high.astype(F32)).astype(BF16)


def dot(a, b, dims):
    return lax.dot_general(a, b, (dims, ((), ())), preferred_element_type=F32)


def dot_wide(a, b, dims):
    high, low = halves(b)
    return dot(a, high, dims) + dot(a, low, dims)


def as_column(row, tokens):
    return jnp.transpose(jnp.broadcast_to(row, (tokens, tokens)))


def row_sums(x):
    return jnp.sum(jnp.transpose(x), axis=0, keepdims=True)


def levels_transposed(tokens):
    source = lax.broadcasted_iota(jnp.int32, (tokens, tokens), 0)
    target = lax.broadcasted_iota(jnp.int32, (tokens, tokens), 1)
    crossed = source ^ target
    levels = jnp.zeros((tokens, tokens), jnp.int32)
    for offset in range(tokens.bit_length() - 1):
        levels = levels + (jnp.right_shift(crossed, offset) > 0).astype(jnp.int32)
    return levels, source <= target


def near_levels(segment_row, tokens):
    levels, causal = levels_transposed(tokens)
    allowed = causal & (as_column(segment_row, tokens) == segment_row)
    return jnp.where(allowed, levels, -1)


def near_weight(levels, weight_ref, head, local_levels):
    weight = jnp.zeros(levels.shape, F32)
    for level in range(local_levels):
        row = weight_ref[level, head : head + 1, :] * level_scale(level)
        weight = jnp.where(levels == level, row, weight)
    return weight


def reach_rows(position_ref, segment_row, gate_refs):
    rows = []
    for bit, gate_ref in enumerate(gate_refs):
        upper = (jnp.right_shift(position_ref[0], bit) & 1) == 1
        hit = jnp.where(segment_row == gate_ref[0:1, :], 1.0, 0.0)
        rows.append(jnp.where(upper, hit, jnp.zeros_like(hit)))
    return rows


def weight_columns(rows, tokens):
    padded = -(-len(rows) // 128) * 128
    stacked = jnp.concatenate(
        rows + [jnp.zeros((padded - len(rows), tokens), F32)], axis=0
    )
    return jnp.transpose(stacked)


def bit_of(position_ref, bit):
    return jnp.right_shift(position_ref[0], bit) & 1


def tail_kernel(segment_ref, key_ref, value_ref, out_ref, *, first, heads, width):
    tokens = key_ref.shape[0]
    segment_row = segment_ref[0:1, :].astype(F32)
    last = segment_row[:, tokens - 1 :]
    keep_row = jnp.where(segment_row == last, 1.0, 0.0)
    for h in range(heads):
        cols = slice((first + h) * width, (first + h + 1) * width)
        turned = (jnp.transpose(key_ref[:, cols].astype(F32)) * keep_row).astype(BF16)
        out_ref[h * width : (h + 1) * width, :] = dot(turned, value_ref[:, cols], ((1,), (0,)))
    out_ref[heads * width :, :] = jnp.broadcast_to(last, (GATE_ROWS, width))


def combine_kernel(position_ref, state_ref, got_ref, out_ref, *half_refs, bit):
    rows = out_ref.shape[0] - GATE_ROWS
    upper = bit_of(position_ref, bit)
    same = jnp.where(state_ref[rows : rows + 1, :] == got_ref[rows : rows + 1, :], 1.0, 0.0)

    @pl.when(upper == 1)
    def _():
        out_ref[:rows, :] = state_ref[:rows, :] + same * got_ref[:rows, :]
        out_ref[rows:, :] = state_ref[rows:, :]

    @pl.when(upper == 0)
    def _():
        out_ref[:rows, :] = got_ref[:rows, :] + same * state_ref[:rows, :]
        out_ref[rows:, :] = got_ref[rows:, :]

    for half_ref in half_refs:
        half = rows // 2
        start = pl.multiple_of(bit_of(position_ref, 0) * half, 8)
        half_ref[:half, :] = out_ref[pl.ds(start, half), :]
        half_ref[half:, :] = out_ref[rows:, :]


def pass_kernel(in_ref, out_ref):
    out_ref[...] = in_ref[...]


def join_kernel(position_ref, mine_ref, other_ref, out_ref):
    half = mine_ref.shape[0] - GATE_ROWS
    parity = bit_of(position_ref, 0)
    out_ref[pl.ds(pl.multiple_of(parity * half, 8), half), :] = mine_ref[:half, :]
    out_ref[pl.ds(pl.multiple_of((1 - parity) * half, 8), half), :] = other_ref[:half, :]
    out_ref[2 * half :, :] = mine_ref[half:, :]


def near_kernel(segment_ref, weight_ref, query_ref, key_ref, value_ref, out_ref, *, first, heads, width):
    tokens = key_ref.shape[0]
    levels = near_levels(segment_ref[0:1, :].astype(F32), tokens)
    for h in range(heads):
        cols = slice((first + h) * width, (first + h + 1) * width)
        scores = dot(key_ref[:, cols], query_ref[:, cols], ((1,), (1,)))
        weight = near_weight(levels, weight_ref, first + h, tokens.bit_length())
        near = (scores * weight).astype(BF16)
        out_ref[:, h * width : (h + 1) * width] = dot(near, value_ref[:, cols], ((0,), (0,)))


def read_kernel(
    position_ref, segment_ref, weight_ref, query_ref, near_ref, gain_ref, grad_ref, *rest, first, heads, width, bits
):
    buckets, outs = rest[:bits], rest[bits:]
    mixed_ref, out_ref = outs[-2:]
    tokens = query_ref.shape[0]
    local_levels = tokens.bit_length()
    segment_row = segment_ref[0:1, :].astype(F32)
    gates = [bucket.at[heads * width :, :] for bucket in buckets]
    reaches = reach_rows(position_ref, segment_row, gates)
    rows = [
        reaches[bit] * weight_ref[local_levels + bit, first + h : first + h + 1, :] * level_scale(local_levels + bit)
        for h in range(heads)
        for bit in range(bits)
    ]
    columns = weight_columns(rows, tokens)
    squares = jnp.zeros((tokens, width), F32)
    project = jnp.zeros((tokens, width), F32)
    for h in range(heads):
        here = slice(h * width, (h + 1) * width)
        cols = slice((first + h) * width, (first + h + 1) * width)
        mixed = near_ref[:, here]
        for bit in range(bits):
            at = h * bits + bit
            read = dot_wide(query_ref[:, cols], buckets[bit][here, :], ((1,), (0,)))
            mixed = mixed + read * columns[:, at : at + 1]
        mixed_ref[:, here] = mixed
        squares = squares + mixed * mixed
        project = project + gain_ref[0:1, cols] * grad_ref[:, cols].astype(F32) * mixed
    square_row, project_row = row_sums(squares), row_sums(project)
    if len(outs) == 3:
        square_row, project_row = outs[0][0:1, :] + square_row, outs[0][1:2, :] + project_row
    out_ref[0:1, :] = square_row
    out_ref[1:2, :] = project_row


def grad_kernel(
    position_ref, segment_ref, weight_ref, sums_ref, query_ref, mixed_ref, gain_ref, grad_ref, *rest, first, heads, width, bits, features
):
    gates = [ref.at[ref.shape[0] - GATE_ROWS :, :] for ref in rest[:bits]]
    outs = rest[len(rest) - bits - 3 :]
    normed_ref, grad_mixed_ref, send_ref, bucket_refs = outs[0], outs[1], outs[2], outs[3:]
    tokens = query_ref.shape[0]
    local_levels = tokens.bit_length()
    segment_row = segment_ref[0:1, :].astype(F32)
    reaches = reach_rows(position_ref, segment_row, gates)
    inverse_row = 1.0 / jnp.sqrt(sums_ref[0:1, :] / features + EPSILON)
    pull_row = sums_ref[1:2, :] / features * inverse_row * inverse_row * inverse_row
    inverse = as_column(inverse_row, tokens)
    pull = as_column(pull_row, tokens)
    for h in range(heads):
        here = slice(h * width, (h + 1) * width)
        cols = slice((first + h) * width, (first + h + 1) * width)
        mixed = mixed_ref[:, here]
        gain = gain_ref[0:1, cols]
        normed_ref[:, cols] = (mixed * inverse * gain).astype(BF16)
        grad_mixed = (gain * grad_ref[:, cols].astype(F32) * inverse - mixed * pull).astype(BF16)
        grad_mixed_ref[:, here] = grad_mixed
        turned = jnp.transpose(query_ref[:, cols].astype(F32))
        for bit in range(bits):
            row = (
                reaches[bit]
                * weight_ref[local_levels + bit, first + h : first + h + 1, :]
                * level_scale(local_levels + bit)
            )
            high, low = halves(turned * row)
            bucket_refs[bit][here, :] = dot(high, grad_mixed, ((1,), (0,))) + dot(low, grad_mixed, ((1,), (0,)))
    half = heads * width // 2
    start = pl.multiple_of((1 - bit_of(position_ref, 0)) * half, 8)
    send_ref[...] = bucket_refs[bits - 1][pl.ds(start, half), :]


def top_kernel(position_ref, bucket_ref, got_ref, out_ref):
    half = out_ref.shape[0]
    start = pl.multiple_of(bit_of(position_ref, 0) * half, 8)
    out_ref[...] = bucket_ref[pl.ds(start, half), :] + got_ref[...]


def gate_factors(position_ref, state_ref, got_ref, bit):
    rows = state_ref.shape[0] - GATE_ROWS
    same = jnp.where(state_ref[rows : rows + 1, :] == got_ref[rows : rows + 1, :], 1.0, 0.0)
    upper = jnp.full_like(same, bit_of(position_ref, bit).astype(F32))
    return upper * same + (1.0 - upper), upper + (1.0 - upper) * same


def back_first_kernel(position_ref, state_ref, got_ref, bucket_ref, half_ref, stay_ref, out_ref, *, bit):
    send, stay = gate_factors(position_ref, state_ref, got_ref, bit)
    half = half_ref.shape[0]
    parity = bit_of(position_ref, 0)
    mine = pl.ds(pl.multiple_of(parity * half, 8), half)
    other = pl.ds(pl.multiple_of((1 - parity) * half, 8), half)
    out_ref[mine, :] = bucket_ref[mine, :] + send * half_ref[...]
    out_ref[other, :] = bucket_ref[other, :]
    stay_ref[mine, :] = stay * half_ref[...]
    stay_ref[other, :] = jnp.zeros_like(half_ref)


def back_kernel(position_ref, state_ref, got_ref, bucket_ref, before_ref, incoming_ref, stay_ref, out_ref, *, bit):
    send, stay = gate_factors(position_ref, state_ref, got_ref, bit)
    carried = before_ref[...] + incoming_ref[...]
    out_ref[...] = bucket_ref[...] + send * carried
    stay_ref[...] = stay * carried


def local_kernel(
    position_ref, segment_ref, weight_ref, query_ref, key_ref, value_ref, grad_mixed_ref, *rest, first, heads, width, bits
):
    buckets = rest[:bits]
    grad_query_ref, grad_key_ref, grad_value_ref, level_ref = rest[len(rest) - 4 :]
    tokens = query_ref.shape[0]
    local_levels = tokens.bit_length()
    segment_row = segment_ref[0:1, :].astype(F32)
    levels = near_levels(segment_row, tokens)
    gates = [bucket.at[heads * width :, :] for bucket in buckets]
    reaches = reach_rows(position_ref, segment_row, gates)
    for h in range(heads):
        here = slice(h * width, (h + 1) * width)
        cols = slice((first + h) * width, (first + h + 1) * width)
        at_head = slice(first + h, first + h + 1)
        query, key, value = query_ref[:, cols], key_ref[:, cols], value_ref[:, cols]
        grad_mixed = grad_mixed_ref[:, here]
        scores = dot(key, query, ((1,), (1,)))
        weight = near_weight(levels, weight_ref, first + h, local_levels)
        near = (scores * weight).astype(BF16)
        grad_near = dot(value, grad_mixed, ((1,), (1,)))
        grad_score = (grad_near * weight).astype(BF16)
        grad_key_ref[:, here] = dot(grad_score, query, ((1,), (0,)))
        grad_value_ref[:, here] = dot(near, grad_mixed, ((1,), (0,)))
        product = grad_near * scores
        for level in range(local_levels):
            total = jnp.sum(jnp.where(levels == level, product, 0.0), axis=0, keepdims=True)
            level_ref[level, at_head, :] = total * level_scale(level)
        grad_query = dot(key, grad_score, ((0,), (0,)))
        query_turned = jnp.transpose(query.astype(F32))
        for bit in range(bits):
            high, low = halves(buckets[bit][here, :])
            back = dot(high, grad_mixed, ((1,), (1,))) + dot(low, grad_mixed, ((1,), (1,)))
            reach = reaches[bit] * level_scale(local_levels + bit)
            grad_query = grad_query + back * (reach * weight_ref[local_levels + bit, at_head, :])
            level_ref[local_levels + bit, at_head, :] = reach * jnp.sum(query_turned * back, axis=0, keepdims=True)
        grad_query_ref[:, cols] = jnp.transpose(grad_query).astype(BF16)


def finish_kernel(
    segment_ref, key_ref, value_ref, grad_key_ref, grad_value_ref, staying_ref, incoming_ref, *rest, first, heads, width
):
    out_key_ref, out_value_ref = rest[len(rest) - 2 :]
    tokens = key_ref.shape[0]
    segment_row = segment_ref[0:1, :].astype(F32)
    keep = as_column(jnp.where(segment_row == segment_row[:, tokens - 1 :], 1.0, 0.0), tokens)
    for h in range(heads):
        here = slice(h * width, (h + 1) * width)
        cols = slice((first + h) * width, (first + h + 1) * width)
        high, low = halves(staying_ref[here, :] + incoming_ref[here, :])
        key, value = key_ref[:, cols], value_ref[:, cols]
        back_key = dot(value, high, ((1,), (1,))) + dot(value, low, ((1,), (1,)))
        back_value = dot(key, high, ((1,), (0,))) + dot(key, low, ((1,), (0,)))
        out_key_ref[:, cols] = (grad_key_ref[:, here] + keep * back_key).astype(BF16)
        out_value_ref[:, cols] = (grad_value_ref[:, here] + keep * back_value).astype(BF16)


class Order:
    last = None


def without_token(kernel, at, *refs, **static):
    return kernel(*refs[:at], *refs[at + 1 :], **static)


def call(order, kernel, name, outs, args, aliases=None, **static):
    position, *arrays = args
    if order.last is not None and not any(order.last is a for a in arrays):
        at = len(arrays) + (position is not None)
        kernel = functools.partial(without_token, kernel, at)
        arrays = arrays + [order.last]
    specs = [pl.BlockSpec(memory_space=pltpu.VMEM)] * len(arrays)
    arrays = [pltpu.with_memory_space_constraint(a, pltpu.VMEM) for a in arrays]
    if position is not None:
        specs, arrays = [pl.BlockSpec(memory_space=pltpu.SMEM)] + specs, [position] + arrays
    result = pl.pallas_call(
        functools.partial(kernel, **static),
        in_specs=specs,
        out_specs=[pl.BlockSpec(memory_space=pltpu.VMEM)] * len(outs),
        out_shape=[pltpu.VMEM(dims, kind) for dims, kind in outs],
        input_output_aliases=aliases or {},
        compiler_params=pltpu.CompilerParams(vmem_limit_bytes=4 << 20),
        name=name,
    )(*arrays)
    order.last = result[-1]
    return result


def stage_kernel(*refs):
    count = (len(refs) - 1) // 2
    copies = [pltpu.make_async_copy(refs[i], refs[count + i], refs[-1].at[i]) for i in range(count)]
    for copy in copies:
        copy.start()
    for copy in copies:
        copy.wait()


def stage(*arrays):
    return pl.pallas_call(
        stage_kernel,
        in_specs=[pl.BlockSpec(memory_space=pl.ANY)] * len(arrays),
        out_specs=[pl.BlockSpec(memory_space=pltpu.VMEM)] * len(arrays),
        out_shape=[pltpu.VMEM(a.shape, a.dtype) for a in arrays],
        scratch_shapes=[pltpu.SemaphoreType.DMA((len(arrays),))],
        compiler_params=pltpu.CompilerParams(vmem_limit_bytes=4 << 20),
        name="stage",
    )(*arrays)


def per_device(queries, keys, values, segment, level_weight, gain, grad_out):
    tokens, width_all = queries.shape
    _, head_count, _ = level_weight.shape
    width = width_all // head_count
    count = lax.axis_size("tm")
    bits = count.bit_length() - 1
    top = bits - 1
    features = width_all * lax.axis_size("head")
    position = lax.axis_index("tm").astype(jnp.int32).reshape(1)
    segment_row = segment.reshape(1, tokens)
    gain_row = gain.reshape(1, width_all)
    chunks = chunk_list(head_count)
    n_chunks = len(chunks)
    wide = ((tokens, width_all), BF16)

    swap_all = [[(i, i ^ (1 << bit)) for i in range(count)] for bit in range(bits)]
    climb = [(i, i + count // 2) for i in range(count // 2)]
    descend = [(b, a) for a, b in climb]

    order = Order()
    run = functools.partial(call, order)
    keys, values = stage(keys, values)
    states = [[None] * bits for _ in chunks]
    got = [[None] * bits for _ in chunks]
    flying = [None] * n_chunks
    half_got = [None] * n_chunks
    near = [None] * n_chunks
    mixed = [None] * n_chunks
    sums = ()

    def message_of(heads):
        return ((heads * width + GATE_ROWS, width), F32)

    for c, (first, heads) in enumerate(chunks):
        (states[c][0],) = run(
            tail_kernel, "tails", [message_of(heads)], (None, segment_row, keys, values), first=first, heads=heads, width=width
        )
        flying[c] = lax.ppermute(states[c][0], "tm", swap_all[0])
    queries, grad_out, level_weight, gain_row = stage(queries, grad_out, level_weight, gain_row)

    def forward_step(c, stage):
        heads = chunks[c][1]
        half = ((heads * width // 2 + GATE_ROWS, width), F32)
        arrived = flying[c]
        if stage < top:
            got[c][stage] = arrived
            outs = [message_of(heads)] + ([half] if stage == top - 1 else [])
            result = run(combine_kernel, "combine", outs, (position, states[c][stage], arrived), bit=stage)
            states[c][stage + 1] = result[0]
            pairs = climb if stage == top - 1 else swap_all[stage + 1]
            flying[c] = lax.ppermute(result[-1], "tm", pairs)
        elif stage == top:
            (half_got[c],) = run(pass_kernel, "pass", [half], (None, arrived))
            flying[c] = lax.ppermute(half_got[c], "tm", swap_all[0])
        else:
            (got[c][top],) = run(join_kernel, "join", [message_of(heads)], (position, half_got[c], arrived))

    def near_step(c):
        first, heads = chunks[c]
        (near[c],) = run(
            near_kernel,
            "near",
            [((tokens, heads * width), F32)],
            (None, segment_row, level_weight, queries, keys, values),
            first=first,
            heads=heads,
            width=width,
        )

    def read_step(c):
        nonlocal sums
        first, heads = chunks[c]
        mixed[c], row_pair = run(
            read_kernel,
            "read",
            [((tokens, heads * width), F32), ((2, tokens), F32)],
            (position, segment_row, level_weight, queries, near[c], gain_row, grad_out, *got[c], *sums),
            first=first,
            heads=heads,
            width=width,
            bits=bits,
        )
        sums = (row_pair,)

    for diagonal in range(n_chunks + bits):
        for stage_at in range(bits + 1):
            c = diagonal - stage_at
            if 0 <= c < n_chunks:
                forward_step(c, stage_at)
                if stage_at == 0:
                    near_step(c)
        if 0 <= diagonal - bits < n_chunks:
            read_step(diagonal - bits)
    totals = lax.psum(sums[0], "head")

    normed = ()
    grad_mixed = [None] * n_chunks
    grad_buckets = [None] * n_chunks
    staying = [None] * n_chunks
    near_grads = [None] * n_chunks
    grad_query = level_out = grad_key = grad_value = None
    order.last = None

    def grad_step(c):
        nonlocal normed
        first, heads = chunks[c]
        rows = heads * width
        args = (position, segment_row, level_weight, totals, queries, mixed[c], gain_row, grad_out, *got[c], *normed)
        outs = run(
            grad_kernel,
            "grads",
            [wide, ((tokens, rows), BF16), ((rows // 2, width), F32)] + [((rows, width), F32)] * bits,
            args,
            {len(args) - 1: 0} if normed else None,
            first=first,
            heads=heads,
            width=width,
            bits=bits,
            features=features,
        )
        normed = (outs[0],)
        grad_mixed[c], grad_buckets[c] = outs[1], outs[3:]
        flying[c] = lax.ppermute(outs[2], "tm", swap_all[0])

    def backward_step(c, stage):
        rows = chunks[c][1] * width
        full = ((rows, width), F32)
        arrived = flying[c]
        bit = top - stage
        if stage == 0:
            (half,) = run(top_kernel, "top", [((rows // 2, width), F32)], (position, grad_buckets[c][top], arrived))
            flying[c] = lax.ppermute(half, "tm", descend)
        elif stage == 1:
            staying[c], outgoing = run(
                back_first_kernel,
                "back",
                [full, full],
                (position, states[c][bit], got[c][bit], grad_buckets[c][bit], arrived),
                bit=bit,
            )
            flying[c] = lax.ppermute(outgoing, "tm", swap_all[bit])
        elif stage < bits:
            staying[c], outgoing = run(
                back_kernel,
                "back",
                [full, full],
                (position, states[c][bit], got[c][bit], grad_buckets[c][bit], staying[c], arrived),
                bit=bit,
            )
            flying[c] = lax.ppermute(outgoing, "tm", swap_all[bit])
        else:
            finish_step(c)

    def local_step(c):
        nonlocal grad_query, level_out
        first, heads = chunks[c]
        rows = heads * width
        args = (position, segment_row, level_weight, queries, keys, values, grad_mixed[c], *got[c])
        aliases = None
        if grad_query is not None:
            aliases = {len(args): 0, len(args) + 1: 3}
            args = args + (grad_query, level_out)
        grad_query, near_key, near_value, level_out = run(
            local_kernel,
            "local",
            [wide, ((tokens, rows), F32), ((tokens, rows), F32), (level_weight.shape, F32)],
            args,
            aliases,
            first=first,
            heads=heads,
            width=width,
            bits=bits,
        )
        near_grads[c] = (near_key, near_value)

    def finish_step(c):
        nonlocal grad_key, grad_value
        first, heads = chunks[c]
        args = (None, segment_row, keys, values, *near_grads[c], staying[c], flying[c])
        aliases = None
        if grad_key is not None:
            aliases = {len(args) - 1: 0, len(args): 1}
            args = args + (grad_key, grad_value)
        grad_key, grad_value = run(
            finish_kernel, "finish", [wide, wide], args, aliases, first=first, heads=heads, width=width
        )

    grad_step(0)
    for diagonal in range(n_chunks + bits):
        if diagonal + 1 < n_chunks:
            grad_step(diagonal + 1)
        for c in range(n_chunks - 1, -1, -1):
            if 0 <= diagonal - c <= bits:
                backward_step(c, diagonal - c)
                if diagonal - c == 1:
                    local_step(c)
    return normed[0], grad_query, grad_key, grad_value, level_out


def solution(mesh):
    placed = (
        P("tm", "head"),
        P("tm", "head"),
        P("tm", "head"),
        P("tm"),
        P(None, "head", "tm"),
        P("head"),
        P("tm", "head"),
    )
    return jax.shard_map(
        per_device,
        mesh=mesh,
        in_specs=placed,
        out_specs=(
            P("tm", "head"),
            P("tm", "head"),
            P("tm", "head"),
            P("tm", "head"),
            P(None, "head", "tm"),
        ),
        check_vma=False,
    )
```
